32 devices in a mesh: rep: 8 (over y, x, core), blk: 4 (over z).
Axes of the slice: x: 2, y: 2, z: 4, core: 2. Of those that a mesh axis runs over, the one named last changes fastest.
Arguments:
- features: bfloat16 [2, 2048, 1024], P(None, 'rep'), may hold values from -0.1875 to 0.1875
- grad_act: bfloat16 [2, 2048, 6144], P(None, 'rep', 'blk'), may hold values from -2.5 to 2.5
- weights: bfloat16 [1024, 6144], P(None, 'blk'), may hold values from -6 to 6
- owner_slot: int32 [4, 24], P('blk'), may hold values from 0 to 23, each once within a row
- factors: float32 [4, 24, 2, 256, 256], P('blk', 'rep'), may hold values from -100 to 250, as said below
- roots: bfloat16 [4, 24, 2, 256, 256], P('blk', 'rep'), may hold values from -1 to 2, as said below
- helper_list: int32 [2, 4, 4], replicated, may hold values from 0 to 23, as said below
Outputs:
- weights_out: bfloat16 [4, 24, 256, 256], P('blk', 'rep')
- roots_out: bfloat16 [4, 24, 2, 256, 256], P('blk', 'rep')
The draws below stay inside these ranges and needn't reach their ends.
Inputs may be any that keep to these rules, and one draw needn't show every extreme that they name: `owner_slot`: each row is a permutation of the slots of one group; slot s belongs to index s // 3 of rep. `factors`: symmetric positive definite. `roots`: Symmetric. `helper_list`: entry [t, h, j] is a factor id as in the reference program, refreshed in step t by index h of blk. In a step every helper has exactly 4 ids, no id appears twice, and no helper has two ids of one group; a group has at most min(6, 4) of its ids in a step.
All inputs are finite; a program needn't handle non-finite values.
Results may differ from the reference program's by a relative error of at most 0.0085.
Values may be sent and summed in bfloat16 or wider, within the bound.
No kernel may reach another device: no remote copies, remote signals or barrier semaphores. Data moves between devices by JAX's collectives and lax.ppermute only.
A program may use at most 128 MiB of HBM per device.

```python
import math
import jax
import jax.numpy as jnp
from jax import lax

BLOCK = 256
OWN = 3
STEPS = 2
NEWTON = 3
SLOTS = 4
GROUPS = 4
NBG = 24
ROWS = 1024
COLS = 6144
TOKENS = 2048
N_REP = 8


def helper_round(key):
    per_owner = 2 * OWN
    top_load = min(per_owner, GROUPS)
    lift = top_load - SLOTS
    half_lift = lift // 2
    subkeys = jax.random.split(key, 3)
    owners = jax.random.permutation(subkeys[0], GROUPS).astype(jnp.int32)
    owner_loads = jnp.full((GROUPS,), SLOTS, jnp.int32)
    owner_loads = owner_loads.at[owners[0]].add(lift).at[owners[1]].add(-lift)
    owner_loads = owner_loads.at[owners[2]].add(half_lift).at[owners[3]].add(-half_lift)
    scores = jax.random.randint(subkeys[1], (GROUPS, per_owner), 0, 1 << 20) * per_owner + jnp.arange(per_owner, dtype=jnp.int32)[None, :]
    local_order = jnp.argsort(scores, axis=1).astype(jnp.int32)
    starts = jnp.cumsum(owner_loads) - owner_loads
    position = jnp.arange(per_owner, dtype=jnp.int32)[None, :]
    is_live = position < owner_loads[:, None]
    ranking = starts[:, None] + position
    helpers = jax.random.permutation(subkeys[2], GROUPS).astype(jnp.int32)
    target = jnp.where(is_live, helpers[ranking % GROUPS], GROUPS)
    slot_index = jnp.where(is_live, ranking // GROUPS, 0)
    factor_ids = jnp.arange(GROUPS, dtype=jnp.int32)[:, None] * per_owner + local_order
    listing = jnp.zeros((GROUPS, SLOTS), jnp.int32)
    return listing.at[target.reshape(-1), slot_index.reshape(-1)].set(factor_ids.reshape(-1), mode='drop')


def draw_helper_list(key, part):
    return jnp.stack([helper_round(jax.random.fold_in(key, 101 + step_index)) for step_index in range(STEPS)])


def draw_factors(key, part):
    subkeys = jax.random.split(jax.random.fold_in(key, 7), 2)
    noise = jax.random.uniform(subkeys[0], (GROUPS, NBG, 2, BLOCK, BLOCK), jnp.float32, -math.sqrt(3.0), math.sqrt(3.0))
    spread = jax.random.uniform(subkeys[1], (GROUPS, NBG, 2, BLOCK), jnp.float32, 0.0, math.log(3.2))
    scales = jnp.exp(spread)
    gram = jnp.einsum('gsnij,gsnkj->gsnik', noise, noise) / BLOCK + 0.5 * jnp.eye(BLOCK, dtype=jnp.float32)
    return gram * scales[..., :, None] * scales[..., None, :]


def draw_roots(key, part):
    subkeys = jax.random.split(jax.random.fold_in(key, 11), 2)
    noise = jax.random.uniform(subkeys[0], (GROUPS, NBG, 2, BLOCK, BLOCK), jnp.float32, -1.0, 1.0)
    diagonal = jnp.exp(jax.random.uniform(subkeys[1], (GROUPS, NBG, 2, BLOCK), jnp.float32, math.log(0.4), math.log(1.2)))
    mirrored = (noise + jnp.swapaxes(noise, -1, -2)) * (0.35 / BLOCK ** 0.5)
    return (mirrored + diagonal[..., None] * jnp.eye(BLOCK, dtype=jnp.float32)).astype(jnp.bfloat16)


def steps_of(rng, shape, pieces, least, largest):
    factor_of, own = 1.0, jax.random.fold_in(rng, 6)
    for dim, blocks in pieces:
        steps = jnp.exp(jax.random.uniform(jax.random.fold_in(own, dim), (blocks,), jnp.float32, least / len(pieces), largest / len(pieces)))
        factor_of = factor_of * jnp.repeat(steps, shape[dim] // blocks).reshape([-1 if axis == dim else 1 for axis in range(len(shape))])
    return factor_of


def bell_draw(key, shape, deviation, bound, shards=(), kind=jnp.bfloat16):
    factor_of = steps_of(key, shape, shards, -0.22, 0.18) if shards else 1.0
    values = jax.random.normal(key, shape, jnp.float32) * deviation * factor_of
    return jnp.minimum(jnp.maximum(values, -bound), bound).astype(kind)


def setup_inputs(seed: int = 0) -> dict:
    key_list = jax.random.split(jax.random.key(seed), 8)
    return {
        "features": bell_draw(key_list[0], (STEPS, TOKENS, ROWS), ROWS ** -0.5, 0.1875, ((1, 8),)),
        "grad_act": bell_draw(key_list[1], (STEPS, TOKENS, COLS), (max(1, 3 * TOKENS // ROWS)) ** -0.5, 2.5, ((1, 8), (2, 4))),
        "weights": bell_draw(key_list[2], (ROWS, COLS), 1.0, 6.0, ((1, 4),)),
        "owner_slot": jax.vmap(lambda own: jax.random.permutation(own, NBG))(jax.random.split(key_list[3], GROUPS)).reshape((GROUPS, NBG)).astype(jnp.int32),
        "factors": draw_factors(jax.random.fold_in(key_list[7], 71), 0),
        "roots": draw_roots(jax.random.fold_in(key_list[7], 71), 0),
        "helper_list": draw_helper_list(jax.random.fold_in(key_list[7], 71), 0),
    }


RIDGE = 0.001
NORM_EPS = 1e-06
DECAY = 0.95
STEP_SIZE = 0.5

def rounded(value):
    return lax.optimization_barrier(value.astype(jnp.bfloat16))

def exact_dot(first, second):
    return jnp.einsum('...ij,...jk->...ik', first, second, precision=lax.Precision.HIGHEST)

def inverse_root(matrices):
    identity = jnp.eye(matrices.shape[-1], dtype=jnp.float32)
    ridged = matrices + RIDGE * identity
    norm_scale = jnp.sqrt(lax.optimization_barrier(jnp.sum(ridged * ridged, axis=(-2, -1), keepdims=True)) + NORM_EPS)
    current = ridged / norm_scale
    result = identity
    for newton_turn in range(NEWTON):
        factor = (5.0 * identity - current) / 4.0
        if newton_turn == 0:
            result = factor * norm_scale ** (-0.25)
        else:
            result = exact_dot(result, factor)
        if newton_turn + 1 < NEWTON:
            square = exact_dot(factor, factor)
            current = exact_dot(exact_dot(square, square), current)
    return rounded(result)

def silu_slope(value):
    sigmoid = jax.nn.sigmoid(value)
    return sigmoid * (1.0 + value * (1.0 - sigmoid))

def group_gradient(features_now, act_group, weight_slots, block_ids):
    block_size = weight_slots.shape[-1]
    slot_count = weight_slots.shape[0]
    token_count, row_count = features_now.shape
    row_blocks = row_count // block_size
    col_blocks = slot_count // row_blocks
    width = col_blocks * block_size
    ordered = jnp.zeros_like(weight_slots).at[block_ids].set(weight_slots)
    dense = ordered.reshape(row_blocks, col_blocks, block_size, block_size).transpose(0, 2, 1, 3).reshape(row_count, width)
    gate_value = jnp.dot(features_now, dense, preferred_element_type=jnp.float32)
    dgate = (act_group.astype(jnp.float32) * silu_slope(gate_value)).astype(jnp.bfloat16)
    per_rep = token_count // N_REP
    feature_parts = features_now.reshape(N_REP, per_rep, row_count)
    dgate_parts = dgate.reshape(N_REP, per_rep, width)

    def add_part(total, pair):
        partial_value = rounded(jnp.dot(pair[0].T, pair[1], preferred_element_type=jnp.float32))
        return (total + partial_value.astype(jnp.float32), 0)
    summed = lax.scan(add_part, jnp.zeros((row_count, width), jnp.float32), (feature_parts, dgate_parts))[0]
    blocks = summed.reshape(row_blocks, block_size, col_blocks, block_size).transpose(0, 2, 1, 3).reshape(slot_count, block_size, block_size)
    return blocks[block_ids]

def reference(features, grad_act, weights, owner_slot, factors, roots, helper_list):
    group_count, slot_count = owner_slot.shape
    block_size = factors.shape[-1]
    step_count, token_count, row_count = features.shape
    row_blocks = row_count // block_size
    col_blocks = slot_count // row_blocks
    width = col_blocks * block_size
    owned = slot_count // N_REP
    per_owner = 2 * owned
    slot_ids = jnp.arange(slot_count, dtype=jnp.int32)
    block_at = jax.vmap(lambda placing: jnp.zeros((slot_count,), jnp.int32).at[placing].set(slot_ids))(owner_slot)
    grid = weights.reshape(row_blocks, block_size, group_count, col_blocks, block_size).transpose(2, 0, 3, 1, 4)
    grid = grid.reshape(group_count, slot_count, block_size, block_size)
    weight_slots = jax.vmap(lambda blocks, index: blocks[index])(grid, block_at)
    current_factors = factors
    current_roots = roots
    for step_index in range(step_count):
        acts = grad_act[step_index].reshape(token_count, group_count, width).transpose(1, 0, 2)
        features_now = features[step_index]
        grads = lax.map(lambda items: group_gradient(features_now, items[0], items[1], items[2]), (acts, weight_slots, block_at))
        grads_low = rounded(grads)
        left_side = rounded(jnp.einsum('gsij,gsjk->gsik', current_roots[:, :, 0].astype(jnp.float32), grads_low.astype(jnp.float32)))
        shaped = jnp.einsum('gsij,gsjk->gsik', left_side.astype(jnp.float32), current_roots[:, :, 1].astype(jnp.float32))
        grad_norm = jnp.sqrt(lax.optimization_barrier(jnp.sum(grads * grads, axis=(-2, -1), keepdims=True)) + NORM_EPS)
        shaped_norm = jnp.sqrt(lax.optimization_barrier(jnp.sum(shaped * shaped, axis=(-2, -1), keepdims=True)) + NORM_EPS)
        weight_slots = rounded(weight_slots.astype(jnp.float32) - STEP_SIZE * (grad_norm / shaped_norm) * shaped)
        left_stat = exact_dot(grads, jnp.swapaxes(grads, -1, -2))
        right_stat = exact_dot(jnp.swapaxes(grads, -1, -2), grads)
        current_factors = DECAY * current_factors + (1.0 - DECAY) * jnp.stack([left_stat, right_stat], axis=2)
        names = helper_list[step_index].reshape(-1)
        owner_pick = (names // per_owner)[:, None]
        local_ids = names % per_owner
        slot_pick = jnp.arange(N_REP, dtype=jnp.int32)[None, :] * owned + (local_ids // 2)[:, None]
        side_pick = (local_ids % 2)[:, None]
        picked = current_factors[owner_pick, slot_pick, side_pick]
        fresh = lax.map(inverse_root, picked)
        current_roots = current_roots.at[owner_pick, slot_pick, side_pick].set(fresh)
    return (weight_slots, current_roots)
```

```python
import functools

import jax
import jax.numpy as jnp
from jax import lax
from jax.experimental import pallas as pl
from jax.experimental.pallas import tpu as pltpu
from jax.sharding import PartitionSpec as P

NEWTON = 3
RIDGE = 0.001
NORM_EPS = 1e-06
DECAY = 0.95
STEP_SIZE = 0.5
VMEM_LIMIT = 28 << 20


VM = pl.BlockSpec(memory_space=pltpu.VMEM)
SM = pl.BlockSpec(memory_space=pltpu.SMEM)


def bf(value):
    return value.astype(jnp.bfloat16)


def mm(first, second, contract=((1,), (0,))):
    return lax.dot_general(
        first, second, (contract, ((), ())), preferred_element_type=jnp.float32
    )


def call(kernel, outs, ins, scratch=(), flops=0, moved=0, name=None):
    specs = [SM if value.dtype == jnp.int32 else VM for value in ins]
    return pl.pallas_call(
        kernel,
        out_shape=[jax.ShapeDtypeStruct(shape, dtype) for shape, dtype in outs],
        in_specs=specs,
        out_specs=[VM] * len(outs),
        scratch_shapes=list(scratch),
        compiler_params=pltpu.CompilerParams(vmem_limit_bytes=VMEM_LIMIT),
        cost_estimate=pl.CostEstimate(flops=flops, bytes_accessed=moved, transcendentals=0),
        name=name,
    )(*ins)


def dgate_of(gate, act):
    sigmoid = 0.5 + 0.5 * jnp.tanh(0.5 * gate)
    slope = sigmoid * (1.0 + gate * (1.0 - sigmoid))
    return bf(act.astype(jnp.float32) * slope)


class Plan:
    def __init__(self, mesh, features, grad_act, owner_slot, factors):
        self.reps = mesh.shape["rep"]
        self.blks = mesh.shape["blk"]
        self.block = factors.shape[-1]
        self.half = self.block // 2
        self.owned = factors.shape[1]
        self.per_owner = 2 * self.owned
        self.slots = owner_slot.shape[1]
        self.tokens = features.shape[1]
        self.rows = features.shape[2]
        self.width = grad_act.shape[2]
        self.row_blocks = self.rows // self.block
        self.col_blocks = self.width // self.block
        self.groups = self.reps // 2
        self.masks = []
        bit = 2
        while bit < self.reps:
            self.masks.append(bit)
            bit *= 2
        self.refresh = min(self.per_owner, self.blks)


def invert_slots(plan, slot_ref, inverse):
    for block in range(plan.slots):
        inverse[slot_ref[0, block]] = block


def place_of(plan, inverse, group, k):
    rank = lax.axis_index("rep")
    slot = (rank ^ (2 * group)) * plan.owned + k
    block = inverse[slot]
    row = block // plan.col_blocks
    return row, block - row * plan.col_blocks


def dgate_own(plan, x_ref, act_ref, w_ref, d_out, t_out):
    size = plan.block
    for i in range(plan.row_blocks):
        t_out[i] = x_ref[:, i * size : (i + 1) * size].T
    for j in range(plan.col_blocks):
        cols = slice(j * size, (j + 1) * size)
        d_out[j] = dgate_of(mm(x_ref[...], w_ref[:, cols]), act_ref[:, cols])


def partials(plan, inverse, left, right, outs):
    size = plan.half
    for group in reversed(range(plan.groups)):
        for k in range(plan.owned):
            row, col = place_of(plan, inverse, group, k)
            total = sum(mm(t[row], d[col]) for t, d in zip(left, right))
            total = bf(total)
            outs[2 * group][k] = total[:size]
            outs[2 * group + 1][k] = total[size:]


def first_kernel(plan, slot_ref, x_ref, act_ref, w_ref, d_own, t_own, *rest):
    outs, (own_w, d_par, t_par, inverse) = rest[: 2 * plan.groups], rest[2 * plan.groups :]
    size = plan.block
    invert_slots(plan, slot_ref, inverse)
    dgate_own(plan, x_ref, act_ref, w_ref, d_par, t_par)
    partials(plan, inverse, (t_own, t_par), (d_own, d_par), outs)
    for k in range(plan.owned):
        row, col = place_of(plan, inverse, 0, k)
        for j in range(plan.col_blocks):

            @pl.when(col == j)
            def _():
                own_w[k] = w_ref[
                    pl.ds(pl.multiple_of(row * size, size), size), j * size : (j + 1) * size
                ]


def second_kernel(plan, slot_ref, *rest):
    count = 2 * plan.groups
    x_refs, act_refs, t_refs = rest[0:2], rest[2:4], rest[4:6]
    pieces = rest[6 : 6 + 2 * count]
    outs = rest[6 + 2 * count : 6 + 3 * count]
    grid, d_one, d_two, inverse = rest[6 + 3 * count :]
    size, half = plan.block, plan.half
    rank = lax.axis_index("rep")
    invert_slots(plan, slot_ref, inverse)
    for core in range(2):
        for group in range(plan.groups):
            for k in range(plan.owned):
                place = (2 * group + core) * plan.owned + k
                base = (core * plan.groups + group) * 2
                grid[place, :half] = pieces[base][k]
                grid[place, half:] = pieces[base + 1][k]
    for j in range(plan.col_blocks):
        cols = slice(j * size, (j + 1) * size)
        column = []
        for i in range(plan.row_blocks):
            slot = slot_ref[0, i * plan.col_blocks + j]
            owner = slot // plan.owned
            column.append(grid[(owner ^ rank) * plan.owned + slot - owner * plan.owned])
        for x_ref, act_ref, d_ref in zip(x_refs, act_refs, (d_one, d_two)):
            gate = sum(
                mm(x_ref[:, i * size : (i + 1) * size], column[i])
                for i in range(plan.row_blocks)
            )
            d_ref[j] = dgate_of(gate, act_ref[:, cols])
    partials(plan, inverse, t_refs, (d_one, d_two), outs)


def gradient(plan, addends, k):
    halves = []
    for half in range(2):
        parts = [ref[k].astype(jnp.float32) for ref in addends[half]]
        halves.append(functools.reduce(jnp.add, parts))
    return jnp.concatenate(halves, axis=0)


def total_square(value):
    return jnp.sum(jnp.sum(value * value, axis=1, keepdims=True), axis=0, keepdims=True)


def updated_weight(plan, grad, q_left, q_right, weight):
    left_side = bf(mm(q_left, bf(grad)))
    shaped = mm(left_side, q_right)
    ratio = jnp.sqrt(total_square(grad) + NORM_EPS) / jnp.sqrt(total_square(shaped) + NORM_EPS)
    return bf(weight.astype(jnp.float32) - STEP_SIZE * ratio * shaped)


def split_addends(refs):
    count = len(refs) // 2
    return refs[:count], refs[count:]


def update_kernel(plan, parts, q_ref, w_ref, *rest):
    addends = split_addends(rest[:parts])
    low, high = rest[parts:]
    for k in range(plan.owned):
        grad = gradient(plan, addends, k)
        fresh = updated_weight(plan, grad, q_ref[0, k, 0], q_ref[0, k, 1], w_ref[k])
        low[k] = fresh[: plan.half]
        high[k] = fresh[plan.half :]


def refresh_list(plan, ids_ref, step, places):
    base = lax.axis_index("blk") * plan.per_owner
    count = jnp.int32(0)
    for n in range(plan.refresh + 1):
        places[n] = 0
    for helper in range(ids_ref.shape[1]):
        for entry in range(ids_ref.shape[2]):
            local = ids_ref[step, helper, entry] - base
            inside = jnp.logical_and(local >= 0, local < plan.per_owner)
            places[jnp.minimum(count, plan.refresh)] = jnp.where(inside, local, 0)
            count = count + inside.astype(jnp.int32)
    return count


def inverse_roots(updated):
    size = updated[0].shape[-1]
    row = lax.broadcasted_iota(jnp.int32, (size, size), 0)
    eye = (row == lax.broadcasted_iota(jnp.int32, (size, size), 1)).astype(jnp.float32)
    ridged = [matrix + RIDGE * eye for matrix in updated]
    norms = [jnp.sqrt(total_square(matrix) + NORM_EPS) for matrix in ridged]
    dev = [matrix * (0.25 / norm) for matrix, norm in zip(ridged, norms)]
    scale = [lax.rsqrt(jnp.sqrt(norm)) for norm in norms]
    low = [bf(e) for e in dev]
    lead, tail = 1.25, [-e for e in dev]
    for turn in range(NEWTON - 1):
        part = [mm(e, e) - 2.5 * d for e, d in zip(low, dev)]
        part_low = [bf(s) for s in part]
        part = [mm(s, s) + 3.125 * d for s, d in zip(part_low, part)]
        part_low = [bf(s) for s in part]
        dev = [mm(s, e) + 2.44140625 * d for s, e, d in zip(part_low, low, dev)]
        low = [bf(e) for e in dev]
        tail = [
            1.25 * v - lead * d - mm(bf(v), e) for v, d, e in zip(tail, dev, low)
        ]
        lead = lead * 1.25
    return [bf(s * (lead * eye + v)) for s, v in zip(scale, tail)]


def statistic(plan, addends, k, side):
    grad = bf(gradient(plan, addends, k))
    return mm(grad, grad, ((1,), (1,))) if side == 0 else mm(grad.T, grad)


def root_kernel(plan, parts, step, ids_ref, f_ref, q_ref, x_one, x_two, *rest):
    addends = split_addends(rest[:parts])
    f_out, q_out, t_one, t_two, places = rest[parts:]
    count = refresh_list(plan, ids_ref, step, places)
    for k in range(plan.owned):
        for side in range(2):
            f_out[2 * k + side] = DECAY * f_ref[0, k, side] + (1.0 - DECAY) * statistic(
                plan, addends, k, side
            )
            q_out[2 * k + side] = q_ref[0, k, side]
    fresh = inverse_roots([f_out[places[n]] for n in range(plan.refresh)])
    for n in range(plan.refresh):

        @pl.when(n < count)
        def _():
            q_out[places[n]] = fresh[n]

    size = plan.block
    for x_ref, t_ref in ((x_one, t_one), (x_two, t_two)):
        for i in range(plan.row_blocks):
            t_ref[i] = x_ref[:, i * size : (i + 1) * size].T


def last_kernel(plan, parts, step, ids_ref, f_ref, q_ref, low_ref, high_ref, *rest):
    addends = split_addends(rest[:parts])
    w_out, q_out, f_new, places = rest[parts:]
    count = refresh_list(plan, ids_ref, step, places)
    for k in range(plan.owned):
        grad = gradient(plan, addends, k)
        weight = jnp.concatenate([low_ref[k], high_ref[k]], axis=0)
        w_out[0, k] = updated_weight(plan, grad, q_ref[2 * k], q_ref[2 * k + 1], weight)
        for side in range(2):
            f_new[2 * k + side] = DECAY * f_ref[2 * k + side] + (1.0 - DECAY) * statistic(
                plan, addends, k, side
            )
            q_out[2 * k + side] = q_ref[2 * k + side]
    fresh = inverse_roots([f_new[places[n]] for n in range(plan.refresh)])
    for n in range(plan.refresh):

        @pl.when(n < count)
        def _():
            q_out[places[n]] = fresh[n]


def swap(plan, value, mask):
    return lax.ppermute(value, "rep", [(i, i ^ mask) for i in range(plan.reps)])


def add_low(first, second):
    return bf(first.astype(jnp.float32) + second.astype(jnp.float32))


def bit_order(groups, order):
    return sorted(groups, key=lambda g: (-bin(g).count("1"), g))


def scatter_sum(plan, outs):
    orders = (plan.masks, plan.masks[::-1])
    state = [{g: outs[2 * g + half] for g in range(plan.groups)} for half in range(2)]
    finals = [[state[half][0]] for half in range(2)]
    for stage in range(len(plan.masks)):
        moved = []
        for half in range(2):
            mask = orders[half][stage]
            bit = mask // 2
            going = bit_order([g for g in state[half] if g & bit], None)
            for g in going:
                moved.append((half, g, bit, mask))
        moved.sort(key=lambda item: -bin(item[1]).count("1"))
        for half, g, bit, mask in moved:
            landed = swap(plan, state[half].pop(g), mask)
            if g == bit:
                finals[half].append(landed)
            else:
                state[half][g ^ bit] = add_low(state[half][g ^ bit], landed)
    return finals[0] + finals[1]


def gather_blocks(plan, low, high):
    orders = (plan.masks[::-1], plan.masks)
    state = [{0: low}, {0: high}]
    for stage in range(len(plan.masks)):
        for half in range(2):
            mask = orders[half][stage]
            for g in list(state[half]):
                state[half][g | (mask // 2)] = swap(plan, state[half][g], mask)
    mine = [state[half][g] for g in range(plan.groups) for half in range(2)]
    return mine + [swap(plan, piece, 1) for piece in mine]


def body(mesh, features, grad_act, weights, owner_slot, factors, roots, helper_list):
    plan = Plan(mesh, features, grad_act, owner_slot, factors)
    size, half, owned = plan.block, plan.half, plan.owned
    low_type, wide = jnp.bfloat16, jnp.float32
    sem = functools.partial
    dots = 2 * plan.tokens * plan.rows * plan.width
    piece = ((owned, half, size), low_type)
    table = ((plan.col_blocks, plan.tokens, size), low_type)
    turned = ((plan.row_blocks, size, plan.tokens), low_type)
    pieces = [piece] * (2 * plan.groups)

    x_own, act_own = features[0], grad_act[0]
    x_par, act_par = swap(plan, x_own, 1), swap(plan, act_own, 1)
    d_own, t_own = call(
        sem(dgate_own, plan), [table, turned], [x_own, act_own, weights], flops=dots, name="gate0"
    )
    x_next, act_next = features[1], grad_act[1]
    x_next_par, act_next_par = swap(plan, x_next, 1), swap(plan, act_next, 1)
    *outs, own_w = call(
        sem(first_kernel, plan),
        pieces + [((owned, size, size), low_type)],
        [owner_slot, x_par, act_par, weights, d_own, t_own],
        [pltpu.VMEM(*table), pltpu.VMEM(*turned), pltpu.SMEM((plan.slots,), jnp.int32)],
        flops=2 * dots,
        name="part0",
    )
    addends = scatter_sum(plan, outs)
    parts = len(addends)
    small = 4 * owned * size**3
    low, high = call(
        sem(update_kernel, plan, parts), [piece, piece], [roots, own_w, *addends], flops=small, name="update0"
    )
    blocks = gather_blocks(plan, low, high)
    listed = pltpu.SMEM((plan.refresh + 1,), jnp.int32)
    f_new, q_new, t_one, t_two = call(
        sem(root_kernel, plan, parts, 0),
        [
            ((plan.per_owner, size, size), wide),
            ((plan.per_owner, size, size), low_type),
            turned,
            turned,
        ],
        [helper_list, factors, roots, x_next, x_next_par, *addends],
        [listed],
        flops=100 * size**3,
        name="roots0",
    )
    outs = call(
        sem(second_kernel, plan),
        pieces,
        [owner_slot, x_next, x_next_par, act_next, act_next_par, t_one, t_two, *blocks],
        [
            pltpu.VMEM((plan.slots, size, size), low_type),
            pltpu.VMEM(*table),
            pltpu.VMEM(*table),
            pltpu.SMEM((plan.slots,), jnp.int32),
        ],
        flops=3 * dots,
        name="part1",
    )
    addends = scatter_sum(plan, outs)
    w_out, q_out = call(
        sem(last_kernel, plan, parts, 1),
        [((1, owned, size, size), low_type), ((plan.per_owner, size, size), low_type)],
        [helper_list, f_new, q_new, low, high, *addends],
        [pltpu.VMEM((plan.per_owner, size, size), wide), listed],
        flops=100 * size**3,
        name="last",
    )
    return w_out, q_out.reshape(1, owned, 2, size, size)


def solution(mesh):
    return jax.shard_map(
        functools.partial(body, mesh),
        mesh=mesh,
        in_specs=(
            P(None, "rep", None),
            P(None, "rep", "blk"),
            P(None, "blk"),
            P("blk", None),
            P("blk", "rep", None, None, None),
            P("blk", "rep", None, None, None),
            P(),
        ),
        out_specs=(P("blk", "rep", None, None), P("blk", "rep", None, None, None)),
        check_vma=False,
    )
```
